512 devices in a mesh: req: 32 (over y_hi, x, core), tp: 16 (over z, y_lo).
Axes of the slice: x: 4, y: 8 (y_hi: 4, y_lo: 2; y = y_hi * 2 + y_lo), z: 8, core: 2. Of those that a mesh axis runs over, the one named last changes fastest.
Arguments:
- hidden: bfloat16 [32, 256, 4096], P('req', None, 'tp'), may hold values from -6 to 6
- norm_gain: bfloat16 [4096], P('tp'), may hold values from 0.5 to 1.5
- w_query: bfloat16 [4096, 2048], P(None, 'tp'), may hold values from -0.09375 to 0.09375
- w_key: bfloat16 [4096, 2048], P(None, 'tp'), may hold values from -0.09375 to 0.09375
- w_value: bfloat16 [4096, 2048], P(None, 'tp'), may hold values from -0.09375 to 0.09375
- w_out: bfloat16 [2048, 4096], P('tp'), may hold values from -0.5 to 0.5
- prefix_keys: bfloat16 [16384, 2048], P('req', 'tp'), may hold values from -1000 to 1000
- prefix_values: bfloat16 [16384, 2048], P('req', 'tp'), may hold values from -6 to 6
- lengths: int32 [32], P('req'), may hold values from 32 to 256, as said below
Outputs:
- attended: bfloat16 [32, 256, 4096], P('req', 'tp')
The draws below stay inside these ranges and needn't reach their ends.
Inputs may be any that keep to these rules, and one draw needn't show every extreme that they name: `lengths`: every request has at least 32 suffix tokens; in every draw some request has exactly 256.
All inputs are finite; a program needn't handle non-finite values.
Results may differ from the reference program's by a relative error of at most 0.029.
Values may be sent and summed in bfloat16 or wider, within the bound.
A program may use at most 64 MiB of HBM per device.

```python
import jax
import jax.numpy as jnp
from jax import lax

D = 4096
HEAD_DIM = 128
SLOT = 256
HEADS = 16
REQS = 32
PREFIX = 16384


def draw_lengths(key, part):
    base = jax.random.randint(key, (REQS,), SLOT // 8, SLOT + 1)
    pick = jax.random.randint(jax.random.fold_in(key, 7), (), 0, REQS)
    return jnp.where(jnp.arange(REQS) == pick, SLOT, base).astype(jnp.int32)


def draw_prefix_keys(key, part):
    shape = (PREFIX, HEADS * HEAD_DIM)
    first = jax.random.fold_in(key, 11)
    values = jnp.clip(jax.random.normal(first, shape, jnp.float32), -6.0, 6.0)
    return values.astype(jnp.bfloat16)


def block_levels(rng, dims, shards, smallest, high):
    level = 1.0
    for dim, parts in shards:
        draws = jax.random.uniform(jax.random.fold_in(jax.random.fold_in(rng, 6), dim), (parts,), jnp.float32, smallest / len(shards), high / len(shards))
        level = level * jnp.repeat(jnp.exp(draws), dims[dim] // parts).reshape((-1,) + (1,) * (len(dims) - 1 - dim))
    return level


def gaussian(rng, shape, deviation, limit, pieces=(), kind=jnp.bfloat16):
    entries = jax.random.normal(rng, shape, jnp.float32) * deviation
    if len(pieces) > 0:
        entries = block_levels(rng, shape, pieces, -0.22, 0.18) * entries
    return jnp.clip(entries, min=-limit, max=limit).astype(kind)


def setup_inputs(seed: int = 0) -> dict:
    keys = jax.random.split(jax.random.key(seed), 10)
    hidden = gaussian(keys[0], (REQS, SLOT, D), 1.0, 6.0, ((0, 32), (2, 16)))
    norm_gain = jnp.clip(1.0 + 0.1 * jax.random.normal(keys[1], (D,), jnp.float32), 0.5, 1.5).astype(jnp.bfloat16)
    w_query = gaussian(keys[2], (D, HEADS * HEAD_DIM), D ** -0.5, 0.09375, ((1, 16),))
    w_key = gaussian(keys[3], (D, HEADS * HEAD_DIM), D ** -0.5, 0.09375, ((1, 16),))
    w_value = gaussian(keys[4], (D, HEADS * HEAD_DIM), D ** -0.5, 0.09375, ((1, 16),))
    w_out = gaussian(keys[5], (HEADS * HEAD_DIM, D), HEAD_DIM ** -0.5, 0.5, ((0, 16),))
    prefix_keys = draw_prefix_keys(jax.random.fold_in(keys[9], 71), 0)
    prefix_values = gaussian(keys[7], (PREFIX, HEADS * HEAD_DIM), 1.0, 6.0, ((0, 32), (1, 16)))
    lengths = draw_lengths(jax.random.fold_in(keys[9], 71), 0)
    return {"hidden": hidden, "norm_gain": norm_gain, "w_query": w_query, "w_key": w_key, "w_value": w_value, "w_out": w_out, "prefix_keys": prefix_keys, "prefix_values": prefix_values, "lengths": lengths}


def rotate(values, angles):
    half = values.shape[-1] // 2
    cosine = jnp.cos(angles)
    sine = jnp.sin(angles)
    first = values[..., :half]
    second = values[..., half:]
    return jnp.concatenate([first * cosine - second * sine, second * cosine + first * sine], axis=-1)

def reference(hidden, norm_gain, w_query, w_key, w_value, w_out, prefix_keys, prefix_values, lengths):
    reqs, slot, width = hidden.shape
    head_dim = HEAD_DIM
    heads = HEADS
    prefix = PREFIX
    x = hidden.astype(jnp.float32)
    normed = (x * lax.rsqrt(lax.optimization_barrier(jnp.mean(x * x, axis=-1, keepdims=True)) + 1e-05) * norm_gain.astype(jnp.float32)).astype(jnp.bfloat16)
    flat = normed.reshape(reqs * slot, width)
    positions = (prefix + jnp.arange(slot)).astype(jnp.float32)
    freq = 10000.0 ** (-2.0 * jnp.arange(head_dim // 2).astype(jnp.float32) / head_dim)
    angles = positions[:, None] * freq[None, :]

    def project(weight):
        out = jnp.dot(flat, weight, preferred_element_type=jnp.float32)
        return out.reshape(reqs, slot, heads, head_dim).transpose(0, 2, 1, 3)
    query = rotate(project(w_query), angles).astype(jnp.bfloat16)
    key_new = rotate(project(w_key), angles).astype(jnp.bfloat16)
    value_new = project(w_value).astype(jnp.bfloat16)
    pre_keys = prefix_keys.astype(jnp.float32).reshape(prefix, heads, head_dim).transpose(1, 0, 2)
    pre_values = prefix_values.astype(jnp.float32).reshape(prefix, heads, head_dim).transpose(1, 0, 2)
    causal = jnp.arange(slot)[:, None] >= jnp.arange(slot)[None, :]
    scale = 1.0 / head_dim ** 0.5
    w_heads = w_out.astype(jnp.float32).reshape(heads, head_dim, width)

    def attend(packed):
        q_req, k_req, v_req, length = packed
        q_f = q_req.astype(jnp.float32)
        s_pre = jnp.einsum('hsd,hpd->hsp', q_f, pre_keys) * scale
        s_new = jnp.einsum('hsd,htd->hst', q_f, k_req.astype(jnp.float32)) * scale
        s_new = jnp.where(causal[None], s_new, -jnp.inf)
        top = jnp.maximum(lax.optimization_barrier(jnp.max(s_pre, axis=-1)), lax.optimization_barrier(jnp.max(s_new, axis=-1)))[..., None]
        p_pre = jnp.exp(s_pre - top).astype(jnp.bfloat16).astype(jnp.float32)
        p_new = jnp.where(causal[None], jnp.exp(s_new - top), 0.0).astype(jnp.bfloat16).astype(jnp.float32)
        total = lax.optimization_barrier(jnp.sum(p_pre, axis=-1)) + lax.optimization_barrier(jnp.sum(p_new, axis=-1))
        acc = jnp.einsum('hsp,hpd->hsd', p_pre, pre_values) + jnp.einsum('hst,htd->hsd', p_new, v_req.astype(jnp.float32))
        context = (acc / total[..., None]).astype(jnp.bfloat16)
        terms = jnp.einsum('hsd,hde->hse', context.astype(jnp.float32), w_heads)
        terms = lax.optimization_barrier(terms.astype(jnp.bfloat16)).astype(jnp.float32)
        summed = lax.optimization_barrier(jnp.sum(terms, axis=0))
        keep = jnp.arange(slot) < length
        return jnp.where(keep[:, None], summed, 0.0).astype(jnp.bfloat16)
    return lax.map(attend, (query, key_new, value_new, lengths))
```

```python
import jax
import jax.numpy as jnp
from jax import lax
from jax.experimental import pallas as pl
from jax.experimental.pallas import tpu as pltpu
from jax.sharding import PartitionSpec as P

NX = 4
NY = 4
NZ = 8
MESH = pl.DeviceIdType.MESH


def where_am_i():
    r = lax.axis_index("req")
    t = lax.axis_index("tp")
    core = lax.rem(r, 2)
    x = lax.rem(lax.div(r, 2), NX)
    y = lax.div(r, 2 * NX)
    z = lax.div(t, 2)
    low = lax.rem(t, 2)
    return r, t, core, x, y, z, low


def neighbours():
    r, t, core, x, y, z, low = where_am_i()

    def req(yy, xx, cc):
        return (yy * NX + xx) * 2 + cc

    return dict(
        xp=(req(y, lax.rem(x + 1, NX), core), t),
        xm=(req(y, lax.rem(x + NX - 1, NX), core), t),
        yp=(req(lax.rem(y + 1, NY), x, core), t),
        ym=(req(lax.rem(y + NY - 1, NY), x, core), t),
        sib=(req(y, x, 1 - core), t),
        zp=(r, lax.rem(z + 1, NZ) * 2 + low),
        zm=(r, lax.rem(z + NZ - 1, NZ) * 2 + low),
        peer=(r, z * 2 + 1 - low),
    )


def greet(ids):
    barrier = pltpu.get_barrier_semaphore()
    for dev in ids:
        pl.semaphore_signal(barrier, inc=1, device_id=dev, device_id_type=MESH)
    pl.semaphore_wait(barrier, len(ids))


def remote(src, dst, send_sem, recv_sem, dev):
    return pltpu.make_async_remote_copy(
        src_ref=src, dst_ref=dst, send_sem=send_sem, recv_sem=recv_sem,
        device_id=dev, device_id_type=MESH,
    )


def gather_kernel(
    h_ref, k_ref, v_ref, hid, keys, vals, peer_s, peer_r, z_s, z_r, ring_s, ring_r, sib_s, sib_r, own_sem
):
    _, _, _, _, _, z, low = where_am_i()
    n = neighbours()
    greet(list(n.values()))
    own = (k_ref, v_ref)
    full = (keys, vals)
    sends = []

    def start(copy):
        copy.start()
        sends.append(copy)

    def block(a, dy, dx):
        return own[a] if dy == 0 and dx == 0 else full[a].at[0, dy, dx]

    def ring_copy(a, src, slot, dev):
        dy, dx = slot
        return remote(src, full[a].at[0, dy, dx], ring_s.at[a, dy, dx], ring_r.at[a, dy, dx], dev)

    def to_y(a, dy, forward):
        slot = ((dy + (NY - 1 if forward else 1)) % NY, 0)
        start(ring_copy(a, block(a, dy, 0), slot, n["yp"] if forward else n["ym"]))

    def to_x(a, dy, dx, forward):
        slot = (dy, (dx + (NX - 1 if forward else 1)) % NX)
        start(ring_copy(a, block(a, dy, dx), slot, n["xp"] if forward else n["xm"]))

    def sib_copy(a, dy, dx):
        return remote(
            block(a, dy, dx), full[a].at[1, dy, dx], sib_s.at[a, dy, dx], sib_r.at[a, dy, dx], n["sib"]
        )

    def to_sib(a, dy, dx):
        start(sib_copy(a, dy, dx))

    def arrived(a, dy, dx):
        ring_copy(a, full[a].at[0, dy, dx], (dy, dx), n["xp"]).wait_recv()

    def shard(dist, unit):
        zz = lax.rem(z + dist + NZ, NZ)
        return hid.at[zz * 2 + (low if unit == 0 else 1 - low)]

    def z_copy(way, step, unit):
        dist = -(step - 1) if way == 0 else step - 1
        src = h_ref if step == 1 and unit == 0 else shard(dist, unit)
        return remote(
            src, shard(dist, unit), z_s.at[way, step - 1, unit], z_r.at[way, step - 1, unit],
            n["zp"] if way == 0 else n["zm"],
        )

    def z_arrived(way, step, unit):
        dist = -step if way == 0 else step
        buf = shard(dist, unit)
        remote(buf, buf, z_s.at[way, step - 1, unit], z_r.at[way, step - 1, unit], n["zp"]).wait_recv()

    def z_step(step):
        for unit in (0, 1):
            for way in (0, 1):
                if step == NZ // 2 and unit != way:
                    continue
                z_arrived(way, step, unit)
                if step + 1 < NZ // 2 or (step + 1 == NZ // 2 and unit == way):
                    start(z_copy(way, step + 1, unit))

    def x_first(dy):
        for a, dx, forward in ((0, NX - 1, True), (1, 1, False), (1, NX - 1, None), (0, 1, None)):
            arrived(a, dy, dx)
            if forward is not None:
                to_x(a, dy, dx, forward)
            to_sib(a, dy, dx)

    def x_second(dy):
        for a in (0, 1):
            arrived(a, dy, 2)
            to_sib(a, dy, 2)

    def y_done(a, dy):
        to_x(a, dy, 0, True)
        to_x(a, dy, 0, False)
        to_sib(a, dy, 0)

    peer = remote(h_ref, hid.at[z * 2 + low], peer_s, peer_r, n["peer"])
    start(peer)
    for way in (0, 1):
        start(z_copy(way, 1, 0))
    for a in (0, 1):
        to_y(a, 0, True)
        to_y(a, 0, False)
        to_x(a, 0, 0, True)
        to_x(a, 0, 0, False)
    locals_ = [
        pltpu.make_async_copy(h_ref, hid.at[z * 2 + low], own_sem.at[0]),
        pltpu.make_async_copy(k_ref, keys.at[0, 0, 0], own_sem.at[1]),
        pltpu.make_async_copy(v_ref, vals.at[0, 0, 0], own_sem.at[2]),
    ]
    for c in locals_:
        c.start()
    for a in (0, 1):
        to_sib(a, 0, 0)

    theirs = hid.at[z * 2 + 1 - low]
    remote(theirs, theirs, peer_s, peer_r, n["peer"]).wait_recv()
    for way in (0, 1):
        start(z_copy(way, 1, 1))
    x_first(0)
    z_step(1)
    for a, dy, forward in ((0, NY - 1, True), (1, 1, False), (1, NY - 1, None), (0, 1, None)):
        arrived(a, dy, 0)
        if forward is not None:
            to_y(a, dy, forward)
        y_done(a, dy)
    z_step(2)
    x_second(0)
    x_first(3)
    z_step(3)
    for a in (0, 1):
        arrived(a, 2, 0)
        y_done(a, 2)
    x_first(1)
    z_step(4)
    x_second(3)
    x_second(1)
    x_first(2)
    x_second(2)
    for a in (0, 1):
        for dy in range(NY):
            for dx in range(NX):
                sib_copy(a, dy, dx).wait_recv()
    for c in locals_:
        c.wait()
    for c in sends:
        c.wait_send()


def gather(hidden, prefix_keys, prefix_values):
    rows, width = prefix_keys.shape
    slots = jax.ShapeDtypeStruct((2, NY, NX, rows, width), prefix_keys.dtype)
    dma = pltpu.SemaphoreType.DMA
    return pl.pallas_call(
        gather_kernel,
        out_shape=(jax.ShapeDtypeStruct((NZ * 2, *hidden.shape), hidden.dtype), slots, slots),
        in_specs=[pl.BlockSpec(memory_space=pltpu.VMEM)] * 3,
        out_specs=(pl.BlockSpec(memory_space=pl.ANY),) * 3,
        scratch_shapes=[
            dma, dma, dma((2, NZ // 2, 2)), dma((2, NZ // 2, 2)),
            dma((2, NY, NX)), dma((2, NY, NX)), dma((2, NY, NX)), dma((2, NY, NX)), dma((3,)),
        ],
        compiler_params=pltpu.CompilerParams(collective_id=0, has_side_effects=True),
        name="gather_all",
    )(hidden, prefix_keys, prefix_values)


def reduce_rows(terms):
    return lax.psum_scatter(terms, "tp", scatter_dimension=0, tiled=True).astype(jnp.float32)


def rotate(values, angles):
    half = values.shape[-1] // 2
    cosine = jnp.cos(angles)
    sine = jnp.sin(angles)
    first = values[..., :half]
    second = values[..., half:]
    return jnp.concatenate(
        [first * cosine - second * sine, second * cosine + first * sine], axis=-1
    )


def on_device(
    hidden, norm_gain, w_query, w_key, w_value, w_out, prefix_keys, prefix_values, lengths
):
    slot, part = hidden.shape[1:]
    shard = jnp.concatenate([hidden[0], jnp.broadcast_to(norm_gain[None], (16, part))])
    hid, keys, values = gather(shard, prefix_keys, prefix_values)
    blocks = hid.shape[0]
    head_dim = w_query.shape[1]
    keys = keys.reshape(-1, head_dim)
    values = values.reshape(-1, head_dim)
    prefix = keys.shape[0]
    x = hid[:, :slot].astype(jnp.float32)
    gain = hid[:, slot : slot + 1].astype(jnp.float32)
    normed = (
        x * lax.rsqrt(jnp.mean(x * x, axis=(0, 2), keepdims=True) + 1e-05) * gain
    ).astype(jnp.bfloat16)

    def project(w):
        return jnp.einsum(
            "tsf,tfd->sd", normed, w.reshape(blocks, part, head_dim), preferred_element_type=jnp.float32
        )

    positions = (prefix + jnp.arange(slot)).astype(jnp.float32)
    freq = 10000.0 ** (-2.0 * jnp.arange(head_dim // 2).astype(jnp.float32) / head_dim)
    angles = positions[:, None] * freq[None, :]
    query = rotate(project(w_query), angles).astype(jnp.bfloat16)
    key_new = rotate(project(w_key), angles).astype(jnp.bfloat16)
    value_new = project(w_value).astype(jnp.bfloat16)
    scale = 1.0 / head_dim**0.5
    causal = jnp.arange(slot)[:, None] >= jnp.arange(slot)[None, :]
    own_scores = jnp.einsum("sd,td->st", query, key_new, preferred_element_type=jnp.float32) * scale
    own_scores = jnp.where(causal, own_scores, -jnp.inf)
    top = jnp.max(own_scores, axis=-1)
    own_weights = jnp.where(causal, jnp.exp(own_scores - top[:, None]), 0.0).astype(jnp.bfloat16)
    total = jnp.sum(own_weights.astype(jnp.float32), axis=-1)
    acc = jnp.dot(own_weights, value_new, preferred_element_type=jnp.float32)
    scores = jnp.einsum("sd,pd->sp", query, keys, preferred_element_type=jnp.float32) * scale
    new_top = jnp.maximum(top, jnp.max(scores, axis=-1))
    fade = jnp.exp(top - new_top)
    weights = jnp.exp(scores - new_top[:, None]).astype(jnp.bfloat16)
    run_total = total * fade + jnp.sum(weights.astype(jnp.float32), axis=-1)
    run_acc = acc * fade[:, None] + jnp.dot(weights, values, preferred_element_type=jnp.float32)
    context = (run_acc / run_total[:, None]).astype(jnp.bfloat16)
    rows = slot // lax.axis_size("tp")
    terms = jnp.dot(context, w_out, preferred_element_type=jnp.float32).astype(jnp.bfloat16)
    summed = reduce_rows(terms)
    index = lax.axis_index("tp") * rows + jnp.arange(rows)
    keep = index < lengths[0]
    return jnp.where(keep[:, None], summed, jnp.zeros_like(summed)).astype(jnp.bfloat16)[None]


def solution(mesh):
    return jax.shard_map(
        on_device,
        mesh=mesh,
        in_specs=(
            P("req", None, "tp"),
            P("tp"),
            P(None, "tp"),
            P(None, "tp"),
            P(None, "tp"),
            P("tp", None),
            P("req", "tp"),
            P("req", "tp"),
            P("req"),
        ),
        out_specs=P("req", "tp", None),
        check_vma=False,
    )
```

```python
import jax
import jax.numpy as jnp
from jax import lax
from jax.experimental import pallas as pl
from jax.experimental.pallas import tpu as pltpu
from jax.sharding import PartitionSpec as P

NX = 4
NY = 4
NZ = 8
MESH = pl.DeviceIdType.MESH


def where_am_i():
    r = lax.axis_index("req")
    t = lax.axis_index("tp")
    core = lax.rem(r, 2)
    x = lax.rem(lax.div(r, 2), NX)
    y = lax.div(r, 2 * NX)
    z = lax.div(t, 2)
    low = lax.rem(t, 2)
    return r, t, core, x, y, z, low


def neighbours():
    r, t, core, x, y, z, low = where_am_i()

    def req(yy, xx, cc):
        return (yy * NX + xx) * 2 + cc

    return dict(
        xp=(req(y, lax.rem(x + 1, NX), core), t),
        xm=(req(y, lax.rem(x + NX - 1, NX), core), t),
        yp=(req(lax.rem(y + 1, NY), x, core), t),
        ym=(req(lax.rem(y + NY - 1, NY), x, core), t),
        sib=(req(y, x, 1 - core), t),
        zp=(r, lax.rem(z + 1, NZ) * 2 + low),
        zm=(r, lax.rem(z + NZ - 1, NZ) * 2 + low),
        peer=(r, z * 2 + 1 - low),
    )


def greet(ids):
    barrier = pltpu.get_barrier_semaphore()
    for dev in ids:
        pl.semaphore_signal(barrier, inc=1, device_id=dev, device_id_type=MESH)
    pl.semaphore_wait(barrier, len(ids))


def remote(src, dst, send_sem, recv_sem, dev):
    return pltpu.make_async_remote_copy(
        src_ref=src, dst_ref=dst, send_sem=send_sem, recv_sem=recv_sem,
        device_id=dev, device_id_type=MESH,
    )


def gather_kernel(
    h_ref, k_ref, v_ref, hid, keys, vals, peer_s, peer_r, z_s, z_r, ring_s, ring_r, sib_s, sib_r, own_sem
):
    _, _, _, _, _, z, low = where_am_i()
    n = neighbours()
    greet(list(n.values()))
    own = (k_ref, v_ref)
    full = (keys, vals)
    sends = []

    def start(copy):
        copy.start()
        sends.append(copy)

    def block(a, dy, dx):
        return own[a] if dy == 0 and dx == 0 else full[a].at[0, dy, dx]

    def ring_copy(a, src, slot, dev):
        dy, dx = slot
        return remote(src, full[a].at[0, dy, dx], ring_s.at[a, dy, dx], ring_r.at[a, dy, dx], dev)

    def to_y(a, dy, forward):
        slot = ((dy + (NY - 1 if forward else 1)) % NY, 0)
        start(ring_copy(a, block(a, dy, 0), slot, n["yp"] if forward else n["ym"]))

    def to_x(a, dy, dx, forward):
        slot = (dy, (dx + (NX - 1 if forward else 1)) % NX)
        start(ring_copy(a, block(a, dy, dx), slot, n["xp"] if forward else n["xm"]))

    def sib_copy(a, dy, dx):
        return remote(
            block(a, dy, dx), full[a].at[1, dy, dx], sib_s.at[a, dy, dx], sib_r.at[a, dy, dx], n["sib"]
        )

    def to_sib(a, dy, dx):
        start(sib_copy(a, dy, dx))

    def arrived(a, dy, dx):
        ring_copy(a, full[a].at[0, dy, dx], (dy, dx), n["xp"]).wait_recv()

    def shard(dist, unit):
        zz = lax.rem(z + dist + NZ, NZ)
        return hid.at[zz * 2 + (low if unit == 0 else 1 - low)]

    def z_copy(way, step, unit):
        dist = -(step - 1) if way == 0 else step - 1
        src = h_ref if step == 1 and unit == 0 else shard(dist, unit)
        return remote(
            src, shard(dist, unit), z_s.at[way, step - 1, unit], z_r.at[way, step - 1, unit],
            n["zp"] if way == 0 else n["zm"],
        )

    def z_arrived(way, step, unit):
        dist = -step if way == 0 else step
        buf = shard(dist, unit)
        remote(buf, buf, z_s.at[way, step - 1, unit], z_r.at[way, step - 1, unit], n["zp"]).wait_recv()

    def z_step(step):
        for unit in (0, 1):
            for way in (0, 1):
                if step == NZ // 2 and unit != way:
                    continue
                z_arrived(way, step, unit)
                if step + 1 < NZ // 2 or (step + 1 == NZ // 2 and unit == way):
                    start(z_copy(way, step + 1, unit))

    def x_first(dy):
        for a, dx, forward in ((0, NX - 1, True), (1, 1, False), (1, NX - 1, None), (0, 1, None)):
            arrived(a, dy, dx)
            if forward is not None:
                to_x(a, dy, dx, forward)
            to_sib(a, dy, dx)

    def x_second(dy):
        for a in (0, 1):
            arrived(a, dy, 2)
            to_sib(a, dy, 2)

    def y_done(a, dy):
        to_x(a, dy, 0, True)
        to_x(a, dy, 0, False)
        to_sib(a, dy, 0)

    peer = remote(h_ref, hid.at[z * 2 + low], peer_s, peer_r, n["peer"])
    start(peer)
    for way in (0, 1):
        start(z_copy(way, 1, 0))
    for a in (0, 1):
        to_y(a, 0, True)
        to_y(a, 0, False)
        to_x(a, 0, 0, True)
        to_x(a, 0, 0, False)
    locals_ = [
        pltpu.make_async_copy(h_ref, hid.at[z * 2 + low], own_sem.at[0]),
        pltpu.make_async_copy(k_ref, keys.at[0, 0, 0], own_sem.at[1]),
        pltpu.make_async_copy(v_ref, vals.at[0, 0, 0], own_sem.at[2]),
    ]
    for c in locals_:
        c.start()
    for a in (0, 1):
        to_sib(a, 0, 0)

    theirs = hid.at[z * 2 + 1 - low]
    remote(theirs, theirs, peer_s, peer_r, n["peer"]).wait_recv()
    for way in (0, 1):
        start(z_copy(way, 1, 1))
    x_first(0)
    z_step(1)
    for a, dy, forward in ((0, NY - 1, True), (1, 1, False), (1, NY - 1, None), (0, 1, None)):
        arrived(a, dy, 0)
        if forward is not None:
            to_y(a, dy, forward)
        y_done(a, dy)
    z_step(2)
    x_second(0)
    x_first(3)
    z_step(3)
    for a in (0, 1):
        arrived(a, 2, 0)
        y_done(a, 2)
    x_first(1)
    z_step(4)
    x_second(3)
    x_second(1)
    x_first(2)
    x_second(2)
    for a in (0, 1):
        for dy in range(NY):
            for dx in range(NX):
                sib_copy(a, dy, dx).wait_recv()
    for c in locals_:
        c.wait()
    for c in sends:
        c.wait_send()


def gather(hidden, prefix_keys, prefix_values):
    rows, width = prefix_keys.shape
    slots = jax.ShapeDtypeStruct((2, NY, NX, rows, width), prefix_keys.dtype)
    dma = pltpu.SemaphoreType.DMA
    return pl.pallas_call(
        gather_kernel,
        out_shape=(jax.ShapeDtypeStruct((NZ * 2, *hidden.shape), hidden.dtype), slots, slots),
        in_specs=[pl.BlockSpec(memory_space=pltpu.VMEM)] * 3,
        out_specs=(pl.BlockSpec(memory_space=pl.ANY),) * 3,
        scratch_shapes=[
            dma, dma, dma((2, NZ // 2, 2)), dma((2, NZ // 2, 2)),
            dma((2, NY, NX)), dma((2, NY, NX)), dma((2, NY, NX)), dma((2, NY, NX)), dma((3,)),
        ],
        compiler_params=pltpu.CompilerParams(collective_id=0, has_side_effects=True),
        name="gather_all",
    )(hidden, prefix_keys, prefix_values)


CUT = 4


def sum_kernel(p_ref, o_ref, got, made, y_send, y_got, z_s, z_r, y_s, y_r):
    _, _, _, _, _, z, low = where_am_i()
    n = neighbours()
    greet([n["zp"], n["zm"], n["peer"]])
    half = NZ // 2
    width = p_ref.shape[-1] // CUT
    sends = []

    def cols(c):
        return slice(c * width, (c + 1) * width)

    def starts_at(way, c):
        return 0 if (c < CUT // 2) == (way == 0) else 1

    def target(way, step):
        dist = half - step
        return lax.rem(z + (dist if way == 0 else NZ - dist), NZ)

    def copy(way, step, c, src):
        return remote(
            src, got.at[way, step, :, :, cols(c)], z_s.at[way, step, c], z_r.at[way, step, c],
            n["zp"] if way == 0 else n["zm"],
        )

    def arrived(way, step, c):
        copy(way, step, c, got.at[way, step, :, :, cols(c)]).wait_recv()
        return got[way, step, :, :, cols(c)].astype(jnp.float32)

    def send(way, step, c):
        first = starts_at(way, c)
        if step == first:
            src = p_ref.at[target(way, step), :, :, cols(c)]
        else:
            total = arrived(way, step - 1, c) + p_ref[target(way, step), :, :, cols(c)].astype(
                jnp.float32
            )
            made[way, step, :, :, cols(c)] = total.astype(made.dtype)
            src = made.at[way, step, :, :, cols(c)]
        one = copy(way, step, c, src)
        one.start()
        sends.append(one)

    for step in range(half):
        order = [(way, c) for c in range(CUT) for way in (0, 1)]
        for way, c in order:
            if step >= starts_at(way, c):
                send(way, step, c)

    def y_copy(c):
        return remote(
            y_send.at[:, cols(c)], y_got.at[:, cols(c)], y_s.at[c], y_r.at[c], n["peer"]
        )

    kept = []
    for c in range(CUT):
        for way in (0, 1):
            copy(way, half - 1, c, got.at[way, half - 1, :, :, cols(c)]).wait_recv()

        def total(side):
            return (
                p_ref[z, side, :, cols(c)].astype(jnp.float32)
                + got[0, half - 1, side, :, cols(c)].astype(jnp.float32)
                + got[1, half - 1, side, :, cols(c)].astype(jnp.float32)
            )

        y_send[:, cols(c)] = total(1 - low).astype(y_send.dtype)
        one = y_copy(c)
        one.start()
        sends.append(one)
        o_ref[:, cols(c)] = total(low)
    for c in range(CUT):
        y_copy(c).wait_recv()
        o_ref[:, cols(c)] += y_got[:, cols(c)].astype(jnp.float32)
    for one in sends:
        one.wait_send()


def reduce_rows(terms):
    slot, width = terms.shape
    rows = slot // (NZ * 2)
    kind = terms.dtype
    dma = pltpu.SemaphoreType.DMA
    vmem = pl.BlockSpec(memory_space=pltpu.VMEM)
    half = NZ // 2
    return pl.pallas_call(
        sum_kernel,
        out_shape=jax.ShapeDtypeStruct((rows, width), jnp.float32),
        in_specs=[vmem],
        out_specs=vmem,
        scratch_shapes=[
            pltpu.VMEM((2, half, 2, rows, width), kind),
            pltpu.VMEM((2, half, 2, rows, width), kind),
            pltpu.VMEM((rows, width), kind),
            pltpu.VMEM((rows, width), kind),
            dma((2, half, CUT)), dma((2, half, CUT)), dma((CUT,)), dma((CUT,)),
        ],
        compiler_params=pltpu.CompilerParams(collective_id=1, has_side_effects=True),
        name="sum_heads",
    )(terms.reshape(NZ, 2, rows, width))


def rotate(values, angles):
    half = values.shape[-1] // 2
    cosine = jnp.cos(angles)
    sine = jnp.sin(angles)
    first = values[..., :half]
    second = values[..., half:]
    return jnp.concatenate(
        [first * cosine - second * sine, second * cosine + first * sine], axis=-1
    )


def on_device(
    hidden, norm_gain, w_query, w_key, w_value, w_out, prefix_keys, prefix_values, lengths
):
    slot, part = hidden.shape[1:]
    shard = jnp.concatenate([hidden[0], jnp.broadcast_to(norm_gain[None], (16, part))])
    hid, keys, values = gather(shard, prefix_keys, prefix_values)
    blocks = hid.shape[0]
    head_dim = w_query.shape[1]
    keys = keys.reshape(-1, head_dim)
    values = values.reshape(-1, head_dim)
    prefix = keys.shape[0]
    x = hid[:, :slot].astype(jnp.float32)
    gain = hid[:, slot : slot + 1].astype(jnp.float32)
    normed = (
        x * lax.rsqrt(jnp.mean(x * x, axis=(0, 2), keepdims=True) + 1e-05) * gain
    ).astype(jnp.bfloat16)

    def project(w):
        return jnp.einsum(
            "tsf,tfd->sd", normed, w.reshape(blocks, part, head_dim), preferred_element_type=jnp.float32
        )

    positions = (prefix + jnp.arange(slot)).astype(jnp.float32)
    freq = 10000.0 ** (-2.0 * jnp.arange(head_dim // 2).astype(jnp.float32) / head_dim)
    angles = positions[:, None] * freq[None, :]
    query = rotate(project(w_query), angles).astype(jnp.bfloat16)
    key_new = rotate(project(w_key), angles).astype(jnp.bfloat16)
    value_new = project(w_value).astype(jnp.bfloat16)
    scale = 1.0 / head_dim**0.5
    causal = jnp.arange(slot)[:, None] >= jnp.arange(slot)[None, :]
    own_scores = jnp.einsum("sd,td->st", query, key_new, preferred_element_type=jnp.float32) * scale
    own_scores = jnp.where(causal, own_scores, -jnp.inf)
    top = jnp.max(own_scores, axis=-1)
    own_weights = jnp.where(causal, jnp.exp(own_scores - top[:, None]), 0.0).astype(jnp.bfloat16)
    total = jnp.sum(own_weights.astype(jnp.float32), axis=-1)
    acc = jnp.dot(own_weights, value_new, preferred_element_type=jnp.float32)
    scores = jnp.einsum("sd,pd->sp", query, keys, preferred_element_type=jnp.float32) * scale
    new_top = jnp.maximum(top, jnp.max(scores, axis=-1))
    fade = jnp.exp(top - new_top)
    weights = jnp.exp(scores - new_top[:, None]).astype(jnp.bfloat16)
    run_total = total * fade + jnp.sum(weights.astype(jnp.float32), axis=-1)
    run_acc = acc * fade[:, None] + jnp.dot(weights, values, preferred_element_type=jnp.float32)
    context = (run_acc / run_total[:, None]).astype(jnp.bfloat16)
    rows = slot // lax.axis_size("tp")
    terms = jnp.dot(context, w_out, preferred_element_type=jnp.float32).astype(jnp.bfloat16)
    summed = reduce_rows(terms)
    index = lax.axis_index("tp") * rows + jnp.arange(rows)
    keep = index < lengths[0]
    return jnp.where(keep[:, None], summed, jnp.zeros_like(summed)).astype(jnp.bfloat16)[None]


def solution(mesh):
    return jax.shard_map(
        on_device,
        mesh=mesh,
        in_specs=(
            P("req", None, "tp"),
            P("tp"),
            P(None, "tp"),
            P(None, "tp"),
            P(None, "tp"),
            P("tp", None),
            P("req", "tp"),
            P("req", "tp"),
            P("req"),
        ),
        out_specs=P("req", "tp", None),
        check_vma=False,
    )
```
